256 devices in a mesh: tm: 256 (over z, y, x, core).
Axes of the slice: x: 4, y: 4, z: 8, core: 2. Of those that a mesh axis runs over, the one named last changes fastest.
Arguments:
- queries: bfloat16 [1024, 32, 640], P('tm'), may hold values from -8 to 8
- keys: bfloat16 [1024, 32, 640], P('tm'), may hold values from -8 to 8
- values: bfloat16 [1024, 32, 640], P('tm'), may hold values from -8 to 8
- out_grad: bfloat16 [1024, 32, 640], P('tm'), may hold values from -8 to 8
- clip_lengths: int32 [128], replicated, may hold values from 1 to 24, 1024 in all
Outputs:
- attended: bfloat16 [1024, 32, 640], P('tm')
- grad_queries: bfloat16 [1024, 32, 640], P('tm')
- grad_keys: bfloat16 [1024, 32, 640], P('tm')
- grad_values: bfloat16 [1024, 32, 640], P('tm')
The draws below stay inside these ranges and needn't reach their ends.
Inputs may be any that keep to these rules, and one draw needn't show every extreme that they name: `clip_lengths`: lengths sum to 1024; the longest clip has exactly 24 frames.
All inputs are finite; a program needn't handle non-finite values.
Results may differ from the reference program's by a relative error of at most 0.0088.
Values may be sent and summed in bfloat16 or wider, within the bound.
No kernel may reach another device: no remote copies, remote signals or barrier semaphores. Data moves between devices by JAX's collectives and lax.ppermute only.
A program may use at most 64 MiB of HBM per device.

```python
import math
import jax
import jax.numpy as jnp
import numpy as np
from jax import lax

HEADS = 10
HEAD = 64
D = 640
TOK = 32
MAXCLIP = 24
FRAMES = 1024
CLIPS = 128


def rough_base(key):
    return jax.random.truncated_normal(jax.random.fold_in(key, 5), -8.0, 8.0, (FRAMES, TOK, D), jnp.float32)


def draw_queries(key, part):
    own_key = jax.random.fold_in(key, 11)
    base = rough_base(own_key)
    return base.astype(jnp.bfloat16)


def draw_keys(key, part):
    own_key = jax.random.fold_in(key, 22)
    base = rough_base(own_key)
    return base.astype(jnp.bfloat16)


def steps_of(stream_key, shape, cuts, smallest, largest):
    factor_of, own = 1.0, jax.random.fold_in(stream_key, 6)
    for dim, parts in cuts:
        steps = jnp.exp(jax.random.uniform(jax.random.fold_in(own, dim), (parts,), jnp.float32, smallest / len(cuts), largest / len(cuts)))
        factor_of = factor_of * jnp.repeat(steps, shape[dim] // parts).reshape([-1 if axis == dim else 1 for axis in range(len(shape))])
    return factor_of


def length_profile(amount, total, limit, skew):
    portions = [(1 << 20) // math.isqrt(standing ** skew) + 1 for standing in range(2, amount + 1)]
    surplus, holding = total - limit - (amount - 1), [1] * (amount - 1)
    while surplus > 0:
        free = [i for i in range(amount - 1) if holding[i] < limit]
        pool, left = sum([portions[i] for i in free]), surplus
        for i in free:
            more = min(limit - holding[i], max(1, left * portions[i] // pool), surplus)
            holding[i] = holding[i] + more
            surplus = surplus - more
    return np.array([limit] + holding)


def uneven(rng, count, total, bound, lean):
    if count == 2:
        one = jax.random.randint(rng, (), max(1, total - bound), min(bound, total - 1) + 1)
        return jnp.stack([one, total - one])
    lengths = jnp.asarray(length_profile(count, total, bound, lean), jnp.int32)
    pairs = (count - 1) // 2
    donor, receiver = lengths[1:1 + 2 * pairs:2], lengths[2:2 + 2 * pairs:2]
    room = jnp.minimum(donor - 1, bound - receiver)
    shifted = jax.random.randint(jax.random.fold_in(rng, 1), (pairs,), 0, 1 << 20) % (room + 1)
    lengths = lengths.at[1:1 + 2 * pairs:2].set(donor - shifted).at[2:2 + 2 * pairs:2].set(receiver + shifted)
    return lengths[jax.random.permutation(jax.random.fold_in(rng, 2), count)]


def centred(key, dims, deviation, bound, split=(), kind=jnp.bfloat16):
    level = steps_of(key, dims, split, -0.22, 0.18) if split else 1.0
    result = jax.random.normal(key, dims, jnp.float32) * deviation * level
    return jnp.minimum(jnp.maximum(result, -bound), bound).astype(kind)


def setup_inputs(seed: int = 0) -> dict:
    arg_keys = jax.random.split(jax.random.key(seed), 6)
    queries = draw_queries(jax.random.fold_in(arg_keys[5], 71), 0)
    keys = draw_keys(jax.random.fold_in(arg_keys[5], 71), 0)
    values = centred(arg_keys[2], (FRAMES, TOK, D), 1.0, 8.0, ((0, 256),))
    out_grad = centred(arg_keys[3], (FRAMES, TOK, D), 1.0, 8.0, ((0, 256),))
    clip_lengths = uneven(arg_keys[4], CLIPS, FRAMES, MAXCLIP, 2).astype(jnp.int32)
    return dict(queries=queries, keys=keys, values=values, out_grad=out_grad, clip_lengths=clip_lengths)


def attend_frame(query, key_cat, value_cat, grad_out):
    score_scale = HEAD ** -0.5
    query_heads = query.astype(jnp.float32).reshape(TOK, HEADS, HEAD)
    key_heads = key_cat.astype(jnp.float32).reshape(2 * TOK, HEADS, HEAD)
    value_heads = value_cat.astype(jnp.float32).reshape(2 * TOK, HEADS, HEAD)
    grad_heads = grad_out.astype(jnp.float32).reshape(TOK, HEADS, HEAD)
    scores = jnp.einsum("qhd,khd->hqk", query_heads, key_heads) * score_scale
    row_max = jnp.max(scores, axis=-1, keepdims=True)
    expos = jnp.exp(scores - row_max)
    attn_prob = expos / jnp.sum(expos, axis=-1, keepdims=True)
    prob_low = lax.optimization_barrier(attn_prob.astype(jnp.bfloat16)).astype(jnp.float32)
    attended = jnp.einsum("hqk,khd->qhd", prob_low, value_heads).reshape(TOK, D).astype(jnp.bfloat16)
    grad_prob = jnp.einsum("qhd,khd->hqk", grad_heads, value_heads)
    grad_value = jnp.einsum("hqk,qhd->khd", prob_low, grad_heads).reshape(2 * TOK, D)
    grad_score = attn_prob * (grad_prob - jnp.sum(attn_prob * grad_prob, axis=-1, keepdims=True)) * score_scale
    score_low = lax.optimization_barrier(grad_score.astype(jnp.bfloat16)).astype(jnp.float32)
    grad_query = jnp.einsum("hqk,khd->qhd", score_low, key_heads).reshape(TOK, D).astype(jnp.bfloat16)
    grad_key = jnp.einsum("hqk,qhd->khd", score_low, query_heads).reshape(2 * TOK, D)
    return attended, grad_query, grad_key, grad_value


def reference(queries, keys, values, out_grad, clip_lengths):
    frame_ids = jnp.arange(FRAMES, dtype=jnp.int32)
    clip_ends = jnp.cumsum(clip_lengths).astype(jnp.int32)
    clip_starts = (clip_ends - clip_lengths).astype(jnp.int32)
    owner = jnp.max(jnp.where(clip_starts[None, :] <= frame_ids[:, None], clip_starts[None, :], 0), axis=1).astype(jnp.int32)
    previous = jnp.maximum(frame_ids - 1, owner).astype(jnp.int32)

    def advance(carry, inputs):
        acc_key, acc_value = carry
        query, grad_out, key_index, prev_index = inputs
        key_cat = jnp.concatenate([keys[key_index], keys[prev_index]], axis=0)
        value_cat = jnp.concatenate([values[key_index], values[prev_index]], axis=0)
        attended, grad_query, grad_key, grad_value = attend_frame(query, key_cat, value_cat, grad_out)
        acc_key = acc_key.at[key_index].add(grad_key[:TOK])
        acc_key = acc_key.at[prev_index].add(grad_key[TOK:])
        acc_value = acc_value.at[key_index].add(grad_value[:TOK])
        acc_value = acc_value.at[prev_index].add(grad_value[TOK:])
        return (acc_key, acc_value), (attended, grad_query)

    zeros = jnp.zeros((FRAMES, TOK, D), jnp.float32)
    (acc_key, acc_value), (attended, grad_query) = lax.scan(advance, (zeros, zeros), (queries, out_grad, owner, previous))
    return attended, grad_query, acc_key.astype(jnp.bfloat16), acc_value.astype(jnp.bfloat16)
```

```python
import functools

import jax
import jax.numpy as jnp
from jax import lax
from jax.experimental import pallas as pl
from jax.experimental.pallas import tpu as pltpu
from jax.sharding import PartitionSpec as P

HEADS = 10
MAXCLIP = 24
F = 4
REACH = 6
HALO = F
REMOTE = F + 1
F32 = jnp.float32
BF16 = jnp.bfloat16
VMEM = pl.BlockSpec(memory_space=pltpu.VMEM)
SMEM = pl.BlockSpec(memory_space=pltpu.SMEM)

OWN, PREV, BACK, LAST, TAKE, META = 0, F, 2 * F, 2 * F + 1, 2 * F + 2, 16


def ring(value, steps):
    count = lax.axis_size("tm")
    return lax.ppermute(value, "tm", [(s, (s + steps) % count) for s in range(count)])


def prep_kernel(lengths_ref, keys_ref, values_ref, meta_ref, open_ref, both_ref):
    clips = lengths_ref.shape[1]
    frames = lax.axis_size("tm") * F
    first = lax.axis_index("tm") * F
    lengths = lengths_ref[...]
    rows = lax.broadcasted_iota(jnp.int32, (clips, clips), 0)
    columns = lax.broadcasted_iota(jnp.int32, (clips, clips), 1)
    upper = jnp.where(rows < columns, 1.0, 0.0).astype(BF16)
    padded = jnp.broadcast_to(lengths.astype(F32), (16, clips)).astype(BF16)
    starts = jnp.dot(padded, upper, preferred_element_type=F32)[:1].astype(jnp.int32)

    def owner_of(frame):
        return jnp.max(jnp.where(starts <= frame, starts, 0))

    owners = [owner_of(first + i) for i in range(F)]
    for i in range(F):
        local = owners[i] - first
        meta_ref[OWN + i] = jnp.where(local >= 0, local, REMOTE)
        before = i - 1 if i else HALO
        meta_ref[PREV + i] = jnp.where(local == i, i, before)
    back = lax.axis_index("tm") - lax.shift_right_logical(owners[0], 2)
    meta_ref[BACK] = jnp.clip(back, 1, REACH)
    last = jnp.clip(owners[F - 1] - first, 0, F - 1)
    meta_ref[LAST] = last
    for k in range(1, REACH + 1):
        ahead = first + F * k
        owner = owner_of(ahead) - first
        mine = (owner >= 0) & (owner < F) & (ahead < frames)
        meta_ref[TAKE + k - 1] = mine.astype(jnp.int32)
    key = keys_ref[last]
    value = values_ref[last]
    open_ref[0] = key
    open_ref[1] = value
    both_ref[0] = key
    both_ref[1] = value
    both_ref[2] = keys_ref[F - 1]
    both_ref[3] = values_ref[F - 1]


def gather_slots(meta_ref, keys_ref, values_ref, both_ref, received, key_slots, value_slots):
    for i in range(F):
        key_slots[i] = keys_ref[i]
        value_slots[i] = values_ref[i]
    key_slots[HALO] = both_ref[2]
    value_slots[HALO] = both_ref[3]
    back = meta_ref[BACK]
    for k in range(1, REACH + 1):
        source = both_ref if k == 1 else received[k - 2]

        @pl.when(back == k)
        def _():
            key_slots[REMOTE] = source[0]
            value_slots[REMOTE] = source[1]


def spread(block, heads, size):
    if heads == 1:
        return block
    lane = lax.broadcasted_iota(jnp.int32, block.shape, 1)
    parts = [
        jnp.where((lane >= h * size) & (lane < (h + 1) * size), block, jnp.zeros_like(block))
        for h in range(heads)
    ]
    return jnp.concatenate(parts, axis=0)


def fold(product, heads, size):
    tokens = product.shape[0] // heads
    lane = lax.broadcasted_iota(jnp.int32, (tokens, product.shape[1]), 1)
    result = product[:tokens]
    for h in range(1, heads):
        result = jnp.where(lane < h * size, result, product[h * tokens : (h + 1) * tokens])
    return result


def contract(a, b, da, db):
    return lax.dot_general(a, b, (((da,), (db,)), ((), ())), preferred_element_type=F32)


def soft(keys, values, q, g, size):
    scale = size ** (-0.5)
    scores = contract(keys, q, 1, 1) * scale
    grad_prob = contract(values, g, 1, 1)
    expos = jnp.exp(scores - jnp.max(scores, axis=0, keepdims=True))
    prob = expos / jnp.sum(expos, axis=0, keepdims=True)
    inner = jnp.sum(prob * grad_prob, axis=0, keepdims=True)
    grad_score = prob * (grad_prob - inner) * scale
    return prob.astype(BF16), grad_score.astype(BF16)


def groups_of(width, size):
    groups, start = [], 0
    while start < width:
        span = min(4 * size, width - start)
        groups.append((start, span))
        start += span
    return groups


def pair(slots, own, prev, start, span):
    return jnp.concatenate(
        [slots[own, :, start : start + span], slots[prev, :, start : start + span]], axis=0
    )


def near_kernel(meta_ref, q_ref, keys_ref, values_ref, g_ref, both_ref, *rest):
    received = rest[: REACH - 1]
    sums_ref, key_slots, value_slots, key_sum, value_sum = rest[REACH - 1 :]
    gather_slots(meta_ref, keys_ref, values_ref, both_ref, received, key_slots, value_slots)
    tokens, width = q_ref.shape[1], q_ref.shape[2]
    size = width // HEADS
    for start, span in groups_of(width, size):
        columns = slice(start, start + span)
        heads = span // size
        key_total = jnp.zeros((tokens, span), F32)
        value_total = jnp.zeros((tokens, span), F32)
        for i in range(F):
            own, prev = meta_ref[OWN + i], meta_ref[PREV + i]
            keys = pair(key_slots, own, prev, start, span)
            values = pair(value_slots, own, prev, start, span)
            q = spread(q_ref[i, :, columns], heads, size)
            g = spread(g_ref[i, :, columns], heads, size)
            prob, grad_score = soft(keys, values, q, g, size)
            rows = 2 * tokens if i == 0 else tokens
            grad_value = contract(prob[:rows], g, 1, 0)
            grad_key = contract(grad_score[:rows], q, 1, 0)
            remote = own == REMOTE
            key_total += jnp.where(remote, grad_key[:tokens], 0.0)
            value_total += jnp.where(remote, grad_value[:tokens], 0.0)
            if i == 0:
                halo = prev == HALO
                sums_ref[2, :, columns] = jnp.where(halo, grad_key[tokens:], 0.0).astype(BF16)
                sums_ref[3, :, columns] = jnp.where(halo, grad_value[tokens:], 0.0).astype(BF16)
        sums_ref[0, :, columns] = key_total.astype(BF16)
        sums_ref[1, :, columns] = value_total.astype(BF16)


def full_kernel(meta_ref, q_ref, keys_ref, values_ref, g_ref, both_ref, *rest):
    received = rest[: REACH - 1]
    attended_ref, grad_q_ref, key_acc, value_acc, key_slots, value_slots, key_sum, value_sum = rest[
        REACH - 1 :
    ]
    gather_slots(meta_ref, keys_ref, values_ref, both_ref, received, key_slots, value_slots)
    key_sum[...] = jnp.zeros_like(key_sum)
    value_sum[...] = jnp.zeros_like(value_sum)
    tokens, width = q_ref.shape[1], q_ref.shape[2]
    size = width // HEADS
    for i in range(F):
        own, prev = meta_ref[OWN + i], meta_ref[PREV + i]
        for start, span in groups_of(width, size):
            columns = slice(start, start + span)
            heads = span // size
            keys = pair(key_slots, own, prev, start, span)
            values = pair(value_slots, own, prev, start, span)
            q = spread(q_ref[i, :, columns], heads, size)
            g = spread(g_ref[i, :, columns], heads, size)
            prob, grad_score = soft(keys, values, q, g, size)
            attended_ref[i, :, columns] = fold(contract(prob, values, 0, 0), heads, size).astype(BF16)
            grad_q_ref[i, :, columns] = fold(contract(grad_score, keys, 0, 0), heads, size).astype(BF16)
            grad_value = contract(prob, g, 1, 0)
            grad_key = contract(grad_score, q, 1, 0)
            key_sum[own, :, columns] += grad_key[:tokens]
            value_sum[own, :, columns] += grad_value[:tokens]
            key_sum[prev, :, columns] += grad_key[tokens:]
            value_sum[prev, :, columns] += grad_value[tokens:]
    for i in range(F):
        key_acc[i] = key_sum[i]
        value_acc[i] = value_sum[i]


def final_kernel(meta_ref, key_acc, value_acc, near_ref, *rest):
    received = rest[: REACH - 1]
    grad_keys_ref, grad_values_ref, key_add, value_add = rest[REACH - 1 :]
    for i in range(F):
        grad_keys_ref[i] = key_acc[i].astype(BF16)
        grad_values_ref[i] = value_acc[i].astype(BF16)
    last = meta_ref[LAST]
    for j, (acc, add, out) in enumerate(
        ((key_acc, key_add, grad_keys_ref), (value_acc, value_add, grad_values_ref))
    ):
        add[...] = acc[last]
        for k in range(1, REACH + 1):
            source = near_ref if k == 1 else received[k - 2]

            @pl.when(meta_ref[TAKE + k - 1] > 0)
            def _():
                add[...] += source[j].astype(F32)

        edge = acc[F - 1] + near_ref[2 + j].astype(F32)
        out[F - 1] = edge.astype(BF16)
        out[last] = add[...].astype(BF16)

        @pl.when(last == F - 1)
        def _():
            out[F - 1] = (add[...] + near_ref[2 + j].astype(F32)).astype(BF16)


def body(queries, keys, values, out_grad, clip_lengths):
    frames, tokens, width = queries.shape
    block = jax.ShapeDtypeStruct((frames, tokens, width), BF16)
    two = jax.ShapeDtypeStruct((2, tokens, width), BF16)
    four = jax.ShapeDtypeStruct((4, tokens, width), BF16)
    meta, opened, both = pl.pallas_call(
        prep_kernel,
        out_shape=(jax.ShapeDtypeStruct((META,), jnp.int32), two, four),
        in_specs=[VMEM] * 3,
        out_specs=(SMEM, VMEM, VMEM),
        name="prep",
    )(clip_lengths.reshape(1, -1), keys, values)
    received = [None] * REACH
    for k in range(REACH, 0, -1):
        received[k - 1] = ring(both if k == 1 else opened, k)
    slots = [pltpu.VMEM((F + 2, tokens, width), BF16)] * 2
    sums = [pltpu.VMEM((F + 2, tokens, width), F32)] * 2
    flops = 2 * 6 * frames * 2 * tokens * tokens * width
    operands = (meta, queries, keys, values, out_grad, *received)
    in_specs = [SMEM] + [VMEM] * (4 + REACH)
    send = pl.pallas_call(
        near_kernel,
        out_shape=four,
        in_specs=in_specs,
        out_specs=VMEM,
        scratch_shapes=slots + sums,
        cost_estimate=pl.CostEstimate(flops=flops, bytes_accessed=1 << 20, transcendentals=0),
        name="near",
    )(*operands)
    pair_send = send[:2]
    returned = [None] * REACH
    for k in range(REACH, 0, -1):
        returned[k - 1] = ring(send if k == 1 else pair_send, -k)
    acc = jax.ShapeDtypeStruct((frames, tokens, width), F32)
    attended, grad_queries, key_acc, value_acc = pl.pallas_call(
        full_kernel,
        out_shape=(block, block, acc, acc),
        in_specs=in_specs,
        out_specs=(VMEM,) * 4,
        scratch_shapes=slots + sums,
        cost_estimate=pl.CostEstimate(flops=4 * flops, bytes_accessed=3 << 20, transcendentals=0),
        name="full",
    )(*operands)
    grad_keys, grad_values = pl.pallas_call(
        final_kernel,
        out_shape=(block, block),
        in_specs=[SMEM] + [VMEM] * (2 + REACH),
        out_specs=(VMEM, VMEM),
        scratch_shapes=[pltpu.VMEM((tokens, width), F32)] * 2,
        name="final",
    )(meta, key_acc, value_acc, *returned)
    return attended, grad_queries, grad_keys, grad_values


def solution(mesh):
    sharded = P("tm", None, None)
    return jax.shard_map(
        body,
        mesh=mesh,
        in_specs=(sharded,) * 4 + (P(),),
        out_specs=(sharded,) * 4,
        check_vma=False,
    )
```

```python
import jax
import jax.numpy as jnp
from jax import lax
from jax.experimental import pallas as pl
from jax.experimental.pallas import tpu as pltpu
from jax.sharding import PartitionSpec as P

HEADS = 10
MAXCLIP = 24
F = 4
REACH = 6
HALO = F
REMOTE = F + 1
F32 = jnp.float32
BF16 = jnp.bfloat16
VMEM = pl.BlockSpec(memory_space=pltpu.VMEM)
SMEM = pl.BlockSpec(memory_space=pltpu.SMEM)

OWN, PREV, BACK, LAST, TAKE, META = 0, F, 2 * F, 2 * F + 1, 2 * F + 2, 16


LIMIT = pltpu.CompilerParams(vmem_limit_bytes=16 << 20)


def ring(value, steps):
    count = lax.axis_size("tm")
    return lax.ppermute(value, "tm", [(s, (s + steps) % count) for s in range(count)])


def prep_kernel(lengths_ref, keys_ref, values_ref, meta_ref, open_ref, both_ref):
    clips = lengths_ref.shape[1]
    frames = lax.axis_size("tm") * F
    first = lax.axis_index("tm") * F
    lengths = lengths_ref[...]
    rows = lax.broadcasted_iota(jnp.int32, (clips, clips), 0)
    columns = lax.broadcasted_iota(jnp.int32, (clips, clips), 1)
    upper = jnp.where(rows < columns, 1.0, 0.0).astype(BF16)
    padded = jnp.broadcast_to(lengths.astype(F32), (16, clips)).astype(BF16)
    starts = jnp.dot(padded, upper, preferred_element_type=F32)[:1].astype(jnp.int32)

    def owner_of(frame):
        return jnp.max(jnp.where(starts <= frame, starts, 0))

    owners = [owner_of(first + i) for i in range(F)]
    for i in range(F):
        local = owners[i] - first
        meta_ref[OWN + i] = jnp.where(local >= 0, local, REMOTE)
        before = i - 1 if i else HALO
        meta_ref[PREV + i] = jnp.where(local == i, i, before)
    back = lax.axis_index("tm") - lax.shift_right_logical(owners[0], 2)
    meta_ref[BACK] = jnp.clip(back, 1, REACH)
    last = jnp.clip(owners[F - 1] - first, 0, F - 1)
    meta_ref[LAST] = last
    for k in range(1, REACH + 1):
        ahead = first + F * k
        owner = owner_of(ahead) - first
        mine = (owner >= 0) & (owner < F) & (ahead < frames)
        meta_ref[TAKE + k - 1] = mine.astype(jnp.int32)
    key = keys_ref[last]
    value = values_ref[last]
    open_ref[0] = key
    open_ref[1] = value
    both_ref[0] = key
    both_ref[1] = value
    both_ref[2] = keys_ref[F - 1]
    both_ref[3] = values_ref[F - 1]


def gather_slots(meta_ref, keys_ref, values_ref, both_ref, received, key_slots, value_slots):
    for i in range(F):
        key_slots[i] = keys_ref[i]
        value_slots[i] = values_ref[i]
    key_slots[HALO] = both_ref[2]
    value_slots[HALO] = both_ref[3]
    back = meta_ref[BACK]
    for k in range(1, REACH + 1):
        source = both_ref if k == 1 else received[k - 2]

        @pl.when(back == k)
        def _():
            key_slots[REMOTE] = source[0]
            value_slots[REMOTE] = source[1]


def spread(block, heads, size):
    if heads == 1:
        return block
    lane = lax.broadcasted_iota(jnp.int32, block.shape, 1)
    parts = [
        jnp.where((lane >= h * size) & (lane < (h + 1) * size), block, jnp.zeros_like(block))
        for h in range(heads)
    ]
    return jnp.concatenate(parts, axis=0)


def fold(product, heads, size):
    tokens = product.shape[0] // heads
    lane = lax.broadcasted_iota(jnp.int32, (tokens, product.shape[1]), 1)
    result = product[:tokens]
    for h in range(1, heads):
        result = jnp.where(lane < h * size, result, product[h * tokens : (h + 1) * tokens])
    return result


def contract(a, b, da, db):
    return lax.dot_general(a, b, (((da,), (db,)), ((), ())), preferred_element_type=F32)


def soft(keys, values, q, g, size):
    scale = size ** (-0.5)
    scores = contract(keys, q, 1, 1) * scale
    grad_prob = contract(values, g, 1, 1)
    expos = jnp.exp(scores - jnp.max(scores, axis=0, keepdims=True))
    prob = expos / jnp.sum(expos, axis=0, keepdims=True)
    inner = jnp.sum(prob * grad_prob, axis=0, keepdims=True)
    grad_score = prob * (grad_prob - inner) * scale
    return prob.astype(BF16), grad_score.astype(BF16)


def groups_of(width, size):
    groups, start = [], 0
    while start < width:
        span = min(4 * size, width - start)
        groups.append((start, span))
        start += span
    return groups


def pair(slots, own, prev, start, span):
    return jnp.concatenate(
        [slots[own, :, start : start + span], slots[prev, :, start : start + span]], axis=0
    )


def near_kernel(meta_ref, q_ref, keys_ref, values_ref, g_ref, both_ref, *rest):
    received = rest[: REACH - 1]
    sums_ref, both_sums_ref, key_slots, value_slots = rest[REACH - 1 :]
    gather_slots(meta_ref, keys_ref, values_ref, both_ref, received, key_slots, value_slots)
    tokens, width = q_ref.shape[1], q_ref.shape[2]
    size = width // HEADS
    for start, span in groups_of(width, size):
        columns = slice(start, start + span)
        heads = span // size
        key_total = jnp.zeros((tokens, span), F32)
        value_total = jnp.zeros((tokens, span), F32)
        for i in range(F):
            own, prev = meta_ref[OWN + i], meta_ref[PREV + i]
            keys = pair(key_slots, own, prev, start, span)
            values = pair(value_slots, own, prev, start, span)
            q = spread(q_ref[i, :, columns], heads, size)
            g = spread(g_ref[i, :, columns], heads, size)
            prob, grad_score = soft(keys, values, q, g, size)
            rows = 2 * tokens if i == 0 else tokens
            grad_value = contract(prob[:rows], g, 1, 0)
            grad_key = contract(grad_score[:rows], q, 1, 0)
            remote = own == REMOTE
            key_total += jnp.where(remote, grad_key[:tokens], 0.0)
            value_total += jnp.where(remote, grad_value[:tokens], 0.0)
            if i == 0:
                halo = prev == HALO
                both_sums_ref[2, :, columns] = jnp.where(halo, grad_key[tokens:], 0.0).astype(BF16)
                both_sums_ref[3, :, columns] = jnp.where(halo, grad_value[tokens:], 0.0).astype(BF16)
        for target in (sums_ref, both_sums_ref):
            target[0, :, columns] = key_total.astype(BF16)
            target[1, :, columns] = value_total.astype(BF16)


def full_kernel(meta_ref, q_ref, keys_ref, values_ref, g_ref, both_ref, *rest):
    received = rest[: REACH - 1]
    attended_ref, grad_q_ref, key_acc, value_acc, key_slots, value_slots, key_sum, value_sum = rest[
        REACH - 1 :
    ]
    gather_slots(meta_ref, keys_ref, values_ref, both_ref, received, key_slots, value_slots)
    key_sum[...] = jnp.zeros_like(key_sum)
    value_sum[...] = jnp.zeros_like(value_sum)
    tokens, width = q_ref.shape[1], q_ref.shape[2]
    size = width // HEADS
    for i in range(F):
        own, prev = meta_ref[OWN + i], meta_ref[PREV + i]
        for start, span in groups_of(width, size):
            columns = slice(start, start + span)
            heads = span // size
            keys = pair(key_slots, own, prev, start, span)
            values = pair(value_slots, own, prev, start, span)
            q = spread(q_ref[i, :, columns], heads, size)
            g = spread(g_ref[i, :, columns], heads, size)
            prob, grad_score = soft(keys, values, q, g, size)
            attended_ref[i, :, columns] = fold(contract(prob, values, 0, 0), heads, size).astype(BF16)
            grad_q_ref[i, :, columns] = fold(contract(grad_score, keys, 0, 0), heads, size).astype(BF16)
            grad_value = contract(prob, g, 1, 0)
            grad_key = contract(grad_score, q, 1, 0)
            key_sum[own, :, columns] += grad_key[:tokens]
            value_sum[own, :, columns] += grad_value[:tokens]
            key_sum[prev, :, columns] += grad_key[tokens:]
            value_sum[prev, :, columns] += grad_value[tokens:]
    for i in range(F):
        key_acc[i] = key_sum[i]
        value_acc[i] = value_sum[i]


def final_kernel(meta_ref, key_acc, value_acc, near_ref, *rest):
    received = rest[: REACH - 1]
    grad_keys_ref, grad_values_ref, key_add, value_add = rest[REACH - 1 :]
    for i in range(F):
        grad_keys_ref[i] = key_acc[i].astype(BF16)
        grad_values_ref[i] = value_acc[i].astype(BF16)
    last = meta_ref[LAST]
    for j, (acc, add, out) in enumerate(
        ((key_acc, key_add, grad_keys_ref), (value_acc, value_add, grad_values_ref))
    ):
        add[...] = acc[last]
        for k in range(1, REACH + 1):
            source = near_ref if k == 1 else received[k - 2]

            @pl.when(meta_ref[TAKE + k - 1] > 0)
            def _():
                add[...] += source[j].astype(F32)

        edge = acc[F - 1] + near_ref[2 + j].astype(F32)
        out[F - 1] = edge.astype(BF16)
        out[last] = add[...].astype(BF16)

        @pl.when(last == F - 1)
        def _():
            out[F - 1] = (add[...] + near_ref[2 + j].astype(F32)).astype(BF16)


def body(queries, keys, values, out_grad, clip_lengths):
    frames, tokens, width = queries.shape
    block = jax.ShapeDtypeStruct((frames, tokens, width), BF16)
    two = jax.ShapeDtypeStruct((2, tokens, width), BF16)
    four = jax.ShapeDtypeStruct((4, tokens, width), BF16)
    meta, opened, both = pl.pallas_call(
        prep_kernel,
        out_shape=(jax.ShapeDtypeStruct((META,), jnp.int32), two, four),
        in_specs=[VMEM] * 3,
        out_specs=(SMEM, VMEM, VMEM),
        compiler_params=LIMIT,
        name="prep",
    )(clip_lengths.reshape(1, -1), keys, values)
    received = [None] * REACH
    for k in range(REACH, 0, -1):
        received[k - 1] = ring(both if k == 1 else opened, k)
    slots = [pltpu.VMEM((F + 2, tokens, width), BF16)] * 2
    sums = [pltpu.VMEM((F + 2, tokens, width), F32)] * 2
    flops = 2 * 6 * frames * 2 * tokens * tokens * width
    operands = (meta, queries, keys, values, out_grad, *received)
    in_specs = [SMEM] + [VMEM] * (4 + REACH)
    sums_out, both_out = pl.pallas_call(
        near_kernel,
        out_shape=(two, four),
        in_specs=in_specs,
        out_specs=(VMEM, VMEM),
        scratch_shapes=slots,
        cost_estimate=pl.CostEstimate(flops=flops, bytes_accessed=1 << 20, transcendentals=0),
        compiler_params=LIMIT,
        name="near",
    )(*operands)
    returned = [None] * REACH
    for k in range(REACH, 0, -1):
        returned[k - 1] = ring(both_out if k == 1 else sums_out, -k)
    acc = jax.ShapeDtypeStruct((frames, tokens, width), F32)
    attended, grad_queries, key_acc, value_acc = pl.pallas_call(
        full_kernel,
        out_shape=(block, block, acc, acc),
        in_specs=in_specs,
        out_specs=(VMEM,) * 4,
        scratch_shapes=slots + sums,
        cost_estimate=pl.CostEstimate(flops=4 * flops, bytes_accessed=3 << 20, transcendentals=0),
        compiler_params=LIMIT,
        name="full",
    )(*operands)
    grad_keys, grad_values = pl.pallas_call(
        final_kernel,
        out_shape=(block, block),
        in_specs=[SMEM] + [VMEM] * (2 + REACH),
        out_specs=(VMEM, VMEM),
        scratch_shapes=[pltpu.VMEM((tokens, width), F32)] * 2,
        compiler_params=LIMIT,
        name="final",
    )(meta, key_acc, value_acc, *returned)
    return attended, grad_queries, grad_keys, grad_values


def solution(mesh):
    sharded = P("tm", None, None)
    return jax.shard_map(
        body,
        mesh=mesh,
        in_specs=(sharded,) * 4 + (P(),),
        out_specs=(sharded,) * 4,
        check_vma=False,
    )
```

```python
import jax
import jax.numpy as jnp
from jax import lax
from jax.experimental import pallas as pl
from jax.experimental.pallas import tpu as pltpu
from jax.sharding import PartitionSpec as P


HEADS = 10
F = 4
C = 2 * F
REACH = 3
HALO = C
REMOTE = C + 1
SLOTS = C + 2
SIZE = 64
STEP = 256
SPAN = 384
REST = 256
WIDTH = HEADS * SIZE
F32 = jnp.float32
BF16 = jnp.bfloat16
VMEM = pl.BlockSpec(memory_space=pltpu.VMEM)
SMEM = pl.BlockSpec(memory_space=pltpu.SMEM)
HBM = pl.BlockSpec(memory_space=pltpu.HBM)
LIMIT = pltpu.CompilerParams(vmem_limit_bytes=20 << 20)

OWN, PREV, BACK, OPEN, TAKE, META = 0, C, 2 * C, 2 * C + 1, 2 * C + 2, 2 * C + 2 + REACH


def ring(value, steps):
    count = lax.axis_size("tm")
    return lax.ppermute(value, "tm", [(s, (s + steps) % count) for s in range(count)])


def swap(value):
    count = lax.axis_size("tm")
    return lax.ppermute(value, "tm", [(s, s ^ 1) for s in range(count)])


def place():
    device = lax.axis_index("tm")
    return lax.shift_right_logical(device, 1), device & 1


def window(core):
    return pl.ds(pl.multiple_of(core * STEP, 128), SPAN)


def prep_kernel(lengths_ref, keys_ref, values_ref, meta_ref, mine_ref, send_ref, frames, sems):
    copies = [
        pltpu.make_async_copy(ref, frames.at[i], sems.at[i])
        for i, ref in enumerate((keys_ref, values_ref))
    ]
    for copy in copies:
        copy.start()
    chip, core = place()
    first = chip * C
    total = lax.axis_size("tm") * F
    clips = lengths_ref.shape[1]
    rows = lax.broadcasted_iota(jnp.int32, (clips, clips), 0)
    columns = lax.broadcasted_iota(jnp.int32, (clips, clips), 1)
    earlier = jnp.where(rows < columns, 1.0, 0.0).astype(BF16)
    lengths = jnp.broadcast_to(lengths_ref[...].astype(F32), (16, clips)).astype(BF16)
    starts = jnp.dot(lengths, earlier, preferred_element_type=F32)[:1].astype(jnp.int32)

    def owner_of(frame):
        return jnp.max(jnp.where(starts <= frame, starts, 0))

    owners = [owner_of(first + i) for i in range(C)]
    for i in range(C):
        local = owners[i] - first
        meta_ref[OWN + i] = jnp.where(local >= 0, local, REMOTE)
        meta_ref[PREV + i] = jnp.where(local == i, i, i - 1 if i else HALO)
    meta_ref[BACK] = jnp.clip(chip - lax.shift_right_logical(owners[0], 3), 1, REACH)
    opened = owners[C - 1] - first
    meta_ref[OPEN] = opened
    for k in range(1, REACH + 1):
        ahead = first + C * k
        owner = owner_of(ahead) - first
        mine = (owner >= 0) & (owner < C) & (ahead < total)
        meta_ref[TAKE + k - 1] = mine.astype(jnp.int32)
    local = opened - core * F
    holds = (local >= 0) & (local < F)
    frame = jnp.clip(local, 0, F - 1)
    for copy in copies:
        copy.wait()
    for target, columns in ((mine_ref, window(core)), (send_ref, window(1 - core))):
        for i in range(2):
            target[i] = jnp.where(holds, frames[i, frame, :, columns], 0).astype(BF16)
            target[2 + i] = jnp.where(core == 1, frames[i, F - 1, :, columns], 0).astype(BF16)


def pack_kernel(q_ref, keys_ref, values_ref, g_ref, after_ref, mine_ref, send_ref, sems):
    core = place()[1]
    copies = []
    for t, (target, side) in enumerate(((send_ref, 1 - core), (mine_ref, core))):
        for i, ref in enumerate((q_ref, keys_ref, values_ref, g_ref)):
            copies.append(
                pltpu.make_async_copy(
                    ref.at[:, :, window(side)], target.at[pl.ds(i * F, F)], sems.at[4 * t + i]
                )
            )
    for copy in copies:
        copy.start()
    for copy in copies:
        copy.wait()


def gather_slots(meta_ref, mine_ref, theirs_ref, received, q, keys, values, g):
    core = place()[1]
    for source, base in ((mine_ref, core * F), (theirs_ref, (1 - core) * F)):
        for i, target in enumerate((q, keys, values, g)):
            for j in range(F):
                target[base + j] = source[i * F + j]
    keys[HALO] = received[0][2]
    values[HALO] = received[0][3]
    back = meta_ref[BACK]
    for k in range(1, REACH + 1):

        @pl.when(back == k)
        def _():
            keys[REMOTE] = received[k - 1][0]
            values[REMOTE] = received[k - 1][1]


def spread(block):
    lane = lax.broadcasted_iota(jnp.int32, block.shape, 1)
    parts = [
        jnp.where((lane >= start) & (lane < start + SIZE), block, jnp.zeros_like(block))
        for start in range(0, block.shape[1], SIZE)
    ]
    return jnp.concatenate(parts, axis=0)


def fold(product):
    heads = product.shape[1] // SIZE
    tokens = product.shape[0] // heads
    lane = lax.broadcasted_iota(jnp.int32, (tokens, product.shape[1]), 1)
    result = product[:tokens]
    for h in range(1, heads):
        result = jnp.where(lane < h * SIZE, result, product[h * tokens : (h + 1) * tokens])
    return result


def contract(a, b, da, db):
    return lax.dot_general(a, b, (((da,), (db,)), ((), ())), preferred_element_type=F32)


def soft(keys, values, q, g):
    scale = SIZE ** (-0.5)
    scores = contract(keys, q, 1, 1) * scale
    grad_prob = contract(values, g, 1, 1)
    expos = jnp.exp(scores - jnp.max(scores, axis=0, keepdims=True))
    prob = expos / jnp.sum(expos, axis=0, keepdims=True)
    inner = jnp.sum(prob * grad_prob, axis=0, keepdims=True)
    grad_score = prob * (grad_prob - inner) * scale
    return prob.astype(BF16), grad_score.astype(BF16)


GROUPS = tuple(
    slice(start, min(start + 4 * SIZE, SPAN)) for start in range(0, SPAN, 4 * SIZE)
)


def pair(slots, own, prev, columns):
    return jnp.concatenate([slots[own, :, columns], slots[prev, :, columns]], axis=0)


def near_kernel(meta_ref, mine_ref, theirs_ref, r1, r2, r3, sums_ref, edge_ref, q, keys, values, g):
    gather_slots(meta_ref, mine_ref, theirs_ref, (r1, r2, r3), q, keys, values, g)
    tokens = q.shape[1]
    for columns in GROUPS:
        span = columns.stop - columns.start
        key_total = jnp.zeros((tokens, span), F32)
        value_total = jnp.zeros((tokens, span), F32)
        for i in range(C):
            own, prev = meta_ref[OWN + i], meta_ref[PREV + i]
            heads_q, heads_g = spread(q[i, :, columns]), spread(g[i, :, columns])
            prob, grad_score = soft(
                pair(keys, own, prev, columns), pair(values, own, prev, columns), heads_q, heads_g
            )
            rows = 2 * tokens if i == 0 else tokens
            grad_value = contract(prob[:rows], heads_g, 1, 0)
            grad_key = contract(grad_score[:rows], heads_q, 1, 0)
            remote = own == REMOTE
            key_total += jnp.where(remote, grad_key[:tokens], 0.0)
            value_total += jnp.where(remote, grad_value[:tokens], 0.0)
            if i == 0:
                halo = prev == HALO
                edge_ref[2, :, columns] = jnp.where(halo, grad_key[tokens:], 0.0).astype(BF16)
                edge_ref[3, :, columns] = jnp.where(halo, grad_value[tokens:], 0.0).astype(BF16)
        for target in (sums_ref, edge_ref):
            target[0, :, columns] = key_total.astype(BF16)
            target[1, :, columns] = value_total.astype(BF16)


def full_kernel(meta_ref, mine_ref, theirs_ref, r1, r2, r3, after_ref, keep_ref, send_ref, touch_ref, *scratch):
    q, keys, values, g, key_sum, value_sum, out = scratch
    gather_slots(meta_ref, mine_ref, theirs_ref, (r1, r2, r3), q, keys, values, g)
    key_sum[...] = jnp.zeros_like(key_sum)
    value_sum[...] = jnp.zeros_like(value_sum)
    tokens = q.shape[1]
    for i in range(C):
        own, prev = meta_ref[OWN + i], meta_ref[PREV + i]
        for columns in GROUPS:
            heads_q, heads_g = spread(q[i, :, columns]), spread(g[i, :, columns])
            key = pair(keys, own, prev, columns)
            value = pair(values, own, prev, columns)
            prob, grad_score = soft(key, value, heads_q, heads_g)
            out[i, :, columns] = fold(contract(prob, value, 0, 0)).astype(BF16)
            out[C + i, :, columns] = fold(contract(grad_score, key, 0, 0)).astype(BF16)
            grad_value = contract(prob, heads_g, 1, 0)
            grad_key = contract(grad_score, heads_q, 1, 0)
            key_sum[own, :, columns] += grad_key[:tokens]
            value_sum[own, :, columns] += grad_value[:tokens]
            key_sum[prev, :, columns] += grad_key[tokens:]
            value_sum[prev, :, columns] += grad_value[tokens:]
    for i in range(C):
        out[2 * C + i] = key_sum[i].astype(BF16)
        out[3 * C + i] = value_sum[i].astype(BF16)
    opened = jnp.maximum(meta_ref[OPEN], 0)
    touch_ref[0] = key_sum[opened]
    touch_ref[1] = value_sum[opened]
    touch_ref[2] = key_sum[C - 1]
    touch_ref[3] = value_sum[C - 1]
    core = place()[1]
    lacking = pl.ds(pl.multiple_of(core * 128, 128), REST)
    for a in range(4):
        for j in range(F):
            keep_ref[a * F + j] = out[a * C + core * F + j]
            send_ref[a * F + j] = out[a * C + (1 - core) * F + j, :, lacking]


def join(core, target, kept, got):
    @pl.when(core == 0)
    def _():
        target[:, :SPAN] = kept
        target[:, SPAN:] = got

    @pl.when(core == 1)
    def _():
        target[:, :STEP] = got
        target[:, STEP:] = kept


def early_kernel(keep_ref, got_ref, attended_ref, grad_q_ref):
    core = place()[1]
    for a, target in enumerate((attended_ref, grad_q_ref)):
        for j in range(F):
            join(core, target.at[j], keep_ref[a * F + j], got_ref[a * F + j])


def touch_kernel(meta_ref, touch_ref, r1, r2, r3, kept_ref, send_ref):
    core = place()[1]
    lacking = pl.ds(pl.multiple_of(core * 128, 128), REST)
    same = meta_ref[OPEN] == C - 1
    for a in range(2):
        edge = r1[2 + a].astype(F32)
        total = touch_ref[a] + jnp.where(same, edge, 0.0)
        for k, r in enumerate((r1, r2, r3)):
            total += jnp.where(meta_ref[TAKE + k] > 0, r[a].astype(F32), 0.0)
        kept_ref[a] = total.astype(BF16)
        kept_ref[2 + a] = (touch_ref[2 + a] + edge).astype(BF16)
    for a in range(4):
        send_ref[a] = kept_ref[a, :, lacking]


def final_kernel(meta_ref, keep_ref, got_ref, touched_ref, touched_got_ref, grad_keys_ref, grad_values_ref):
    core = place()[1]
    local = meta_ref[OPEN] - core * F
    for a, target in enumerate((grad_keys_ref, grad_values_ref)):
        for j in range(F):
            join(core, target.at[j], keep_ref[(2 + a) * F + j], got_ref[(2 + a) * F + j])

        @pl.when(core == 1)
        def _():
            join(core, target.at[F - 1], touched_ref[2 + a], touched_got_ref[2 + a])

        @pl.when((local >= 0) & (local < F))
        def _():
            join(core, target.at[local], touched_ref[a], touched_got_ref[a])


def call(kernel, operands, outs, in_specs, out_specs, scratch=(), flops=0, size=0):
    return pl.pallas_call(
        kernel,
        out_shape=outs,
        in_specs=in_specs,
        out_specs=out_specs,
        scratch_shapes=list(scratch),
        compiler_params=LIMIT,
        cost_estimate=pl.CostEstimate(flops=flops, bytes_accessed=size, transcendentals=0),
    )(*operands)


def step(queries, keys, values, out_grad, clip_lengths):
    tokens = queries.shape[1]
    queries, keys, values, out_grad = (
        pltpu.with_memory_space_constraint(a, pltpu.HBM) for a in (queries, keys, values, out_grad)
    )

    def shape(count, columns, dtype=BF16):
        return jax.ShapeDtypeStruct((count, tokens, columns), dtype)

    def room(count, dtype=BF16):
        return pltpu.VMEM((count, tokens, SPAN), dtype)

    meta, own_edge, send_edge = call(
        prep_kernel,
        (clip_lengths.reshape(1, -1), keys, values),
        (jax.ShapeDtypeStruct((META,), jnp.int32), shape(4, SPAN), shape(4, SPAN)),
        [VMEM, HBM, HBM],
        (SMEM, VMEM, VMEM),
        [pltpu.VMEM((2, F, tokens, WIDTH), BF16), pltpu.SemaphoreType.DMA((2,))],
        size=1 << 20,
    )
    got_edge = swap(send_edge)
    edge = own_edge + got_edge
    opened = own_edge[:2] + got_edge[:2]
    far = ring(opened, 6), ring(opened, 4)
    received = (ring(edge, 2), far[1], far[0])
    mine, send = call(
        pack_kernel,
        (queries, keys, values, out_grad, edge),
        (shape(4 * F, SPAN), shape(4 * F, SPAN)),
        [HBM] * 4 + [VMEM],
        (VMEM, VMEM),
        [pltpu.SemaphoreType.DMA((8,))],
        size=2 << 20,
    )
    theirs = swap(send)
    slots = [room(C), room(SLOTS), room(SLOTS), room(C)]
    operands = (meta, mine, theirs, *received)
    flops = 24 * C * tokens * tokens * SPAN
    sums, edge_sums = call(
        near_kernel,
        operands,
        (shape(2, SPAN), shape(4, SPAN)),
        [SMEM] + [VMEM] * 5,
        (VMEM, VMEM),
        slots,
        flops,
        2 << 20,
    )
    far = ring(sums, -6), ring(sums, -4)
    returned = (ring(edge_sums, -2), far[1], far[0])
    keep, send_out, touch = call(
        full_kernel,
        (*operands, sums),
        (shape(4 * F, SPAN), shape(4 * F, REST), shape(4, SPAN, F32)),
        [SMEM] + [VMEM] * 6,
        (VMEM,) * 3,
        slots + [room(SLOTS, F32), room(SLOTS, F32), room(4 * C)],
        4 * flops,
        4 << 20,
    )
    got_out = swap(send_out)
    attended, grad_queries = call(
        early_kernel, (keep, got_out), (shape(F, WIDTH),) * 2, [VMEM] * 2, (VMEM,) * 2, size=1 << 20
    )
    touched, send_touched = call(
        touch_kernel,
        (meta, touch, *returned),
        (shape(4, SPAN), shape(4, REST)),
        [SMEM] + [VMEM] * 4,
        (VMEM,) * 2,
        size=1 << 20,
    )
    grad_keys, grad_values = call(
        final_kernel,
        (meta, keep, got_out, touched, swap(send_touched)),
        (shape(F, WIDTH),) * 2,
        [SMEM] + [VMEM] * 4,
        (VMEM,) * 2,
        size=1 << 20,
    )
    return attended, grad_queries, grad_keys, grad_values


def solution(mesh):
    sharded = P("tm", None, None)
    return jax.shard_map(
        step,
        mesh=mesh,
        in_specs=(sharded,) * 4 + (P(),),
        out_specs=(sharded,) * 4,
        check_vma=False,
    )
```

```python
import jax
import jax.numpy as jnp
from jax import lax
from jax.experimental import pallas as pl
from jax.experimental.pallas import tpu as pltpu
from jax.sharding import PartitionSpec as P


HEADS = 10
F = 4
C = 2 * F
REACH = 3
HALO = C
REMOTE = C + 1
SLOTS = C + 2
SIZE = 64
STEP = 256
SPAN = 384
REST = 256
WIDTH = HEADS * SIZE
F32 = jnp.float32
BF16 = jnp.bfloat16
VMEM = pl.BlockSpec(memory_space=pltpu.VMEM)
SMEM = pl.BlockSpec(memory_space=pltpu.SMEM)
HBM = pl.BlockSpec(memory_space=pltpu.HBM)
LIMIT = pltpu.CompilerParams(vmem_limit_bytes=20 << 20)

OWN, PREV, BACK, OPEN, TAKE, META = 0, C, 2 * C, 2 * C + 1, 2 * C + 2, 2 * C + 2 + REACH


def ring(value, steps):
    count = lax.axis_size("tm")
    return lax.ppermute(value, "tm", [(s, (s + steps) % count) for s in range(count)])


def swap(value):
    count = lax.axis_size("tm")
    return lax.ppermute(value, "tm", [(s, s ^ 1) for s in range(count)])


def place():
    device = lax.axis_index("tm")
    return lax.shift_right_logical(device, 1), device & 1


def window(core):
    return pl.ds(pl.multiple_of(core * STEP, 128), SPAN)


def prep_kernel(clips_ref, keys_ref, values_ref, meta_ref, mine_ref, send_ref, lengths_ref, frames, sems):
    count = pltpu.make_async_copy(clips_ref, lengths_ref, sems.at[2])
    count.start()
    copies = [
        pltpu.make_async_copy(ref, frames.at[i], sems.at[i])
        for i, ref in enumerate((keys_ref, values_ref))
    ]
    for copy in copies:
        copy.start()
    chip, core = place()
    first = chip * C
    total = lax.axis_size("tm") * F
    clips = lengths_ref.shape[1]
    rows = lax.broadcasted_iota(jnp.int32, (clips, clips), 0)
    columns = lax.broadcasted_iota(jnp.int32, (clips, clips), 1)
    earlier = jnp.where(rows < columns, 1.0, 0.0).astype(BF16)
    count.wait()
    lengths = jnp.broadcast_to(lengths_ref[...].astype(F32), (16, clips)).astype(BF16)
    starts = jnp.dot(lengths, earlier, preferred_element_type=F32)[:1].astype(jnp.int32)

    def owner_of(frame):
        return jnp.max(jnp.where(starts <= frame, starts, 0))

    owners = [owner_of(first + i) for i in range(C)]
    for i in range(C):
        local = owners[i] - first
        meta_ref[OWN + i] = jnp.where(local >= 0, local, REMOTE)
        meta_ref[PREV + i] = jnp.where(local == i, i, i - 1 if i else HALO)
    meta_ref[BACK] = jnp.clip(chip - lax.shift_right_logical(owners[0], 3), 1, REACH)
    opened = owners[C - 1] - first
    meta_ref[OPEN] = opened
    for k in range(1, REACH + 1):
        ahead = first + C * k
        owner = owner_of(ahead) - first
        mine = (owner >= 0) & (owner < C) & (ahead < total)
        meta_ref[TAKE + k - 1] = mine.astype(jnp.int32)
    local = opened - core * F
    holds = (local >= 0) & (local < F)
    frame = jnp.clip(local, 0, F - 1)
    for copy in copies:
        copy.wait()
    for target, columns in ((mine_ref, window(core)), (send_ref, window(1 - core))):
        for i in range(2):
            target[i] = jnp.where(holds, frames[i, frame, :, columns], 0).astype(BF16)
            target[2 + i] = jnp.where(core == 1, frames[i, F - 1, :, columns], 0).astype(BF16)


def pack_kernel(q_ref, keys_ref, values_ref, g_ref, after_ref, mine_ref, send_ref, sems):
    core = place()[1]
    copies = []
    for t, (target, side) in enumerate(((send_ref, 1 - core), (mine_ref, core))):
        for i, ref in enumerate((q_ref, keys_ref, values_ref, g_ref)):
            copies.append(
                pltpu.make_async_copy(
                    ref.at[:, :, window(side)], target.at[pl.ds(i * F, F)], sems.at[4 * t + i]
                )
            )
    for copy in copies:
        copy.start()
    for copy in copies:
        copy.wait()


UNITS = C + C // 2
UNIT = 4 * SIZE
HALF = UNIT // 2


def frames_of(unit):
    return (unit,) if unit < C else (2 * (unit - C), 2 * (unit - C) + 1)


def unit_of(load, unit):
    if unit < C:
        return load(unit, slice(0, UNIT))
    return jnp.concatenate([load(i, slice(UNIT, SPAN)) for i in frames_of(unit)], axis=1)


def spread(block):
    lane = lax.broadcasted_iota(jnp.int32, block.shape, 1)
    parts = [
        jnp.where((lane >= start) & (lane < start + SIZE), block, jnp.zeros_like(block))
        for start in range(0, block.shape[1], SIZE)
    ]
    return jnp.concatenate(parts, axis=0)


def fold(product):
    heads = product.shape[1] // SIZE
    tokens = product.shape[0] // heads
    lane = lax.broadcasted_iota(jnp.int32, (tokens, HALF), 1)
    parts = []
    for start in range(0, product.shape[1], HALF):
        h = start // SIZE
        columns = slice(start, start + HALF)
        low = product[h * tokens : (h + 1) * tokens, columns]
        high = product[(h + 1) * tokens : (h + 2) * tokens, columns]
        parts.append(jnp.where(lane < SIZE, low, high))
    return jnp.concatenate(parts, axis=1)


def contract(a, b, da, db):
    return lax.dot_general(a, b, (((da,), (db,)), ((), ())), preferred_element_type=F32)


SCALE = SIZE ** (-0.5)


def local_kernel(meta_ref, mine_ref, theirs_ref, qs, gs, own_k, own_v, prev_k, prev_v, s_prev, d_prev, slots):
    core = place()[1]
    for source, base in ((mine_ref, core * F), (theirs_ref, (1 - core) * F)):
        for a in range(4):
            for j in range(F):
                slots[a, base + j] = source[a * F + j]
    own = [jnp.minimum(meta_ref[OWN + i], C - 1) for i in range(C)]
    prev = [jnp.minimum(meta_ref[PREV + i], C - 1) for i in range(C)]
    for u in range(UNITS):
        qs[u] = spread(unit_of(lambda i, columns: slots[0, i, :, columns], u))
        gs[u] = spread(unit_of(lambda i, columns: slots[3, i, :, columns], u))
        own_k[u] = unit_of(lambda i, columns: slots[1, own[i], :, columns], u)
        own_v[u] = unit_of(lambda i, columns: slots[2, own[i], :, columns], u)
        prev_k[u] = unit_of(lambda i, columns: slots[1, prev[i], :, columns], u)
        prev_v[u] = unit_of(lambda i, columns: slots[2, prev[i], :, columns], u)
    for u in range(UNITS):
        s_prev[u] = contract(prev_k[u], qs[u], 1, 1) * SCALE
        d_prev[u] = contract(prev_v[u], gs[u], 1, 1)


def farther(meta_ref, r1, r2, r3, which):
    back = meta_ref[BACK]
    return jnp.where(back == 1, r1[which], jnp.where(back == 2, r2[which], r3[which]))


def own_rows(meta_ref, local, far, u):
    def load(i, columns):
        here = local[u] if u < C else local[u, :, (i % 2) * HALF : (i % 2 + 1) * HALF]
        return jnp.where(meta_ref[OWN + i] == REMOTE, far[:, columns], here)

    return unit_of(load, u)


def prev_rows(meta_ref, local, halo, u):
    if u not in (0, C):
        return local[u]
    outside = meta_ref[PREV] == HALO
    if u == 0:
        return jnp.where(outside, halo[:, :UNIT], local[u])
    left = jnp.where(outside, halo[:, UNIT:], local[u, :, :HALF])
    return jnp.concatenate([left, local[u, :, HALF:]], axis=1)


def near_kernel(
    meta_ref, r1, r2, r3, qs, gs, own_k, own_v, prev_k, prev_v, s_prev, d_prev,
    sums_ref, edge_ref, prob_ref, grad_ref, scores, grads,
):
    tokens = r1.shape[1]
    far_k, far_v = farther(meta_ref, r1, r2, r3, 0), farther(meta_ref, r1, r2, r3, 1)
    for u in range(UNITS):
        scores[u, :tokens] = contract(own_rows(meta_ref, own_k, far_k, u), qs[u], 1, 1) * SCALE
        grads[u, :tokens] = contract(own_rows(meta_ref, own_v, far_v, u), gs[u], 1, 1)
        if u in (0, C):
            scores[u, tokens:] = contract(prev_rows(meta_ref, prev_k, r1[2], u), qs[u], 1, 1) * SCALE
            grads[u, tokens:] = contract(prev_rows(meta_ref, prev_v, r1[3], u), gs[u], 1, 1)
        else:
            scores[u, tokens:] = s_prev[u]
            grads[u, tokens:] = d_prev[u]
    for u in range(UNITS):
        score, grad_prob = scores[u], grads[u]
        expos = jnp.exp(score - jnp.max(score, axis=0, keepdims=True))
        prob = expos * (1.0 / jnp.sum(expos, axis=0, keepdims=True))
        inner = jnp.sum(prob * grad_prob, axis=0, keepdims=True)
        prob_ref[u] = prob.astype(BF16)
        grad_ref[u] = (prob * (grad_prob - inner) * SCALE).astype(BF16)
    lane = lax.broadcasted_iota(jnp.int32, (tokens, UNIT // 2), 1)
    width = UNIT // 2

    def kept(ref, u):
        flags = [meta_ref[OWN + i] == REMOTE for i in frames_of(u)]
        block = ref[u, :tokens]
        if u < C:
            return jnp.where(flags[0], block, jnp.zeros_like(block))
        inside = ((lane < SIZE) & flags[0]) | ((lane >= SIZE) & flags[1])
        return jnp.where(inside, block, jnp.zeros_like(block))

    halo = meta_ref[PREV] == HALO
    for j, (ref, other) in enumerate(((grad_ref, qs), (prob_ref, gs))):
        first = jnp.concatenate([kept(ref, u) for u in range(C)], axis=1)
        total = contract(first, other[:C].reshape(C * width, UNIT), 1, 0).astype(BF16)
        second = jnp.concatenate([kept(ref, u) for u in range(C, UNITS)], axis=1)
        pairs = contract(second, other[C:].reshape((UNITS - C) * width, UNIT), 1, 0)
        rest = (pairs[:, :HALF] + pairs[:, HALF:]).astype(BF16)
        for target in (sums_ref, edge_ref):
            target[j, :, :UNIT] = total
            target[j, :, UNIT:] = rest
        left = contract(ref[0, tokens:], other[0], 1, 0)
        right = contract(ref[C, tokens:], other[C], 1, 0)[:, :HALF]
        edge_ref[2 + j, :, :UNIT] = jnp.where(halo, left, 0.0).astype(BF16)
        edge_ref[2 + j, :, UNIT:] = jnp.where(halo, right, 0.0).astype(BF16)


def full_kernel(
    meta_ref, r1, r2, r3, qs, gs, own_k, own_v, prev_k, prev_v, prob_ref, grad_ref,
    keep_ref, send_ref, touch_ref, out, key_part, value_part, key_sum, value_sum,
):
    tokens = r1.shape[1]
    far_k, far_v = farther(meta_ref, r1, r2, r3, 0), farther(meta_ref, r1, r2, r3, 1)

    def place_unit(target, base, u, rows, block):
        if u < C:
            target[base + u, rows, :UNIT] = block
        else:
            for n, i in enumerate(frames_of(u)):
                target[base + i, rows, UNIT:] = block[:, n * HALF : (n + 1) * HALF]

    everything = slice(None)
    for u in range(UNITS):
        key = jnp.concatenate(
            [own_rows(meta_ref, own_k, far_k, u), prev_rows(meta_ref, prev_k, r1[2], u)], axis=0
        )
        value = jnp.concatenate(
            [own_rows(meta_ref, own_v, far_v, u), prev_rows(meta_ref, prev_v, r1[3], u)], axis=0
        )
        attended = fold(contract(prob_ref[u], value, 0, 0)).astype(BF16)
        grad_q = fold(contract(grad_ref[u], key, 0, 0)).astype(BF16)
        place_unit(out, 0, u, everything, attended)
        place_unit(out, C, u, everything, grad_q)
        place_unit(value_part, 0, u, everything, contract(prob_ref[u], gs[u], 1, 0))
        place_unit(key_part, 0, u, everything, contract(grad_ref[u], qs[u], 1, 0))
    for part, total in ((key_part, key_sum), (value_part, value_sum)):
        for i in range(C):
            here = jnp.where(meta_ref[PREV + i] == i, part[i, tokens:], 0.0)
            if i + 1 < C:
                here += jnp.where(meta_ref[PREV + i + 1] == i, part[i + 1, tokens:], 0.0)
            total[i] = here
    for i in range(C):
        own = meta_ref[OWN + i]
        key_sum[own] += key_part[i, :tokens]
        value_sum[own] += value_part[i, :tokens]
    for i in range(C):
        out[2 * C + i] = key_sum[i].astype(BF16)
        out[3 * C + i] = value_sum[i].astype(BF16)
    opened = jnp.maximum(meta_ref[OPEN], 0)
    touch_ref[0] = key_sum[opened]
    touch_ref[1] = value_sum[opened]
    touch_ref[2] = key_sum[C - 1]
    touch_ref[3] = value_sum[C - 1]
    core = place()[1]
    lacking = pl.ds(pl.multiple_of(core * 128, 128), REST)
    for a in range(4):
        for j in range(F):
            keep_ref[a * F + j] = out[a * C + core * F + j]
            send_ref[a * F + j] = out[a * C + (1 - core) * F + j, :, lacking]


def join(core, target, kept, got):
    @pl.when(core == 0)
    def _():
        target[:, :SPAN] = kept
        target[:, SPAN:] = got

    @pl.when(core == 1)
    def _():
        target[:, :STEP] = got
        target[:, STEP:] = kept


def early_kernel(keep_ref, got_ref, attended_ref, grad_q_ref):
    core = place()[1]
    for a, target in enumerate((attended_ref, grad_q_ref)):
        for j in range(F):
            join(core, target.at[j], keep_ref[a * F + j], got_ref[a * F + j])


def touch_kernel(meta_ref, touch_ref, r1, r2, r3, kept_ref, send_ref):
    core = place()[1]
    lacking = pl.ds(pl.multiple_of(core * 128, 128), REST)
    same = meta_ref[OPEN] == C - 1
    for a in range(2):
        edge = r1[2 + a].astype(F32)
        total = touch_ref[a] + jnp.where(same, edge, 0.0)
        for k, r in enumerate((r1, r2, r3)):
            total += jnp.where(meta_ref[TAKE + k] > 0, r[a].astype(F32), 0.0)
        kept_ref[a] = total.astype(BF16)
        kept_ref[2 + a] = (touch_ref[2 + a] + edge).astype(BF16)
    for a in range(4):
        send_ref[a] = kept_ref[a, :, lacking]


def final_kernel(meta_ref, keep_ref, got_ref, touched_ref, touched_got_ref, grad_keys_ref, grad_values_ref):
    core = place()[1]
    local = meta_ref[OPEN] - core * F
    for a, target in enumerate((grad_keys_ref, grad_values_ref)):
        for j in range(F):
            join(core, target.at[j], keep_ref[(2 + a) * F + j], got_ref[(2 + a) * F + j])

        @pl.when(core == 1)
        def _():
            join(core, target.at[F - 1], touched_ref[2 + a], touched_got_ref[2 + a])

        @pl.when((local >= 0) & (local < F))
        def _():
            join(core, target.at[local], touched_ref[a], touched_got_ref[a])


def call(kernel, operands, outs, in_specs, out_specs, scratch=(), flops=0, size=0):
    return pl.pallas_call(
        kernel,
        out_shape=outs,
        in_specs=in_specs,
        out_specs=out_specs,
        scratch_shapes=list(scratch),
        compiler_params=LIMIT,
        cost_estimate=pl.CostEstimate(flops=flops, bytes_accessed=size, transcendentals=0),
    )(*operands)


def step(queries, keys, values, out_grad, clip_lengths):
    tokens = queries.shape[1]
    queries, keys, values, out_grad = (
        pltpu.with_memory_space_constraint(a, pltpu.HBM) for a in (queries, keys, values, out_grad)
    )

    def shape(count, columns, dtype=BF16):
        return jax.ShapeDtypeStruct((count, tokens, columns), dtype)

    def room(count, dtype=BF16):
        return pltpu.VMEM((count, tokens, SPAN), dtype)

    meta, own_edge, send_edge = call(
        prep_kernel,
        (pltpu.with_memory_space_constraint(clip_lengths.reshape(1, -1), pltpu.HBM), keys, values),
        (jax.ShapeDtypeStruct((META,), jnp.int32), shape(4, SPAN), shape(4, SPAN)),
        [HBM, HBM, HBM],
        (SMEM, VMEM, VMEM),
        [
            pltpu.VMEM((1, clip_lengths.shape[0]), jnp.int32),
            pltpu.VMEM((2, F, tokens, WIDTH), BF16),
            pltpu.SemaphoreType.DMA((3,)),
        ],
        size=1 << 20,
    )
    got_edge = swap(send_edge)
    edge = own_edge + got_edge
    opened = own_edge[:2] + got_edge[:2]
    far = ring(opened, 6), ring(opened, 4)
    received = (ring(edge, 2), far[1], far[0])
    mine, send = call(
        pack_kernel,
        (queries, keys, values, out_grad, edge),
        (shape(4 * F, SPAN), shape(4 * F, SPAN)),
        [HBM] * 4 + [VMEM],
        (VMEM, VMEM),
        [pltpu.SemaphoreType.DMA((8,))],
        size=2 << 20,
    )
    theirs = swap(send)
    wide = jax.ShapeDtypeStruct((UNITS, UNIT // 2, UNIT), BF16)
    rows = jax.ShapeDtypeStruct((UNITS, tokens, UNIT), BF16)
    half = jax.ShapeDtypeStruct((UNITS, tokens, UNIT // 2), F32)
    local = call(
        local_kernel,
        (meta, mine, theirs),
        (wide, wide, rows, rows, rows, rows, half, half),
        [SMEM] + [VMEM] * 2,
        (VMEM,) * 8,
        [pltpu.VMEM((4, C, tokens, SPAN), BF16)],
        size=4 << 20,
    )
    soft = jax.ShapeDtypeStruct((UNITS, 2 * tokens, UNIT // 2), BF16)
    flops = 24 * C * tokens * tokens * SPAN
    sums, edge_sums, prob, grad_score = call(
        near_kernel,
        (meta, *received, *local),
        (shape(2, SPAN), shape(4, SPAN), soft, soft),
        [SMEM] + [VMEM] * 11,
        (VMEM,) * 4,
        [pltpu.VMEM((UNITS, 2 * tokens, UNIT // 2), F32)] * 2,
        flops,
        2 << 20,
    )
    far = ring(sums, -6), ring(sums, -4)
    returned = (ring(edge_sums, -2), far[1], far[0])
    keep, send_out, touch = call(
        full_kernel,
        (meta, *received, *local[:6], prob, grad_score),
        (shape(4 * F, SPAN), shape(4 * F, REST), shape(4, SPAN, F32)),
        [SMEM] + [VMEM] * 11,
        (VMEM,) * 3,
        [room(4 * C)]
        + [pltpu.VMEM((C, 2 * tokens, SPAN), F32)] * 2
        + [room(SLOTS, F32), room(SLOTS, F32)],
        4 * flops,
        4 << 20,
    )
    got_out = swap(send_out)
    attended, grad_queries = call(
        early_kernel, (keep, got_out), (shape(F, WIDTH),) * 2, [VMEM] * 2, (VMEM,) * 2, size=1 << 20
    )
    touched, send_touched = call(
        touch_kernel,
        (meta, touch, *returned),
        (shape(4, SPAN), shape(4, REST)),
        [SMEM] + [VMEM] * 4,
        (VMEM,) * 2,
        size=1 << 20,
    )
    grad_keys, grad_values = call(
        final_kernel,
        (meta, keep, got_out, touched, swap(send_touched)),
        (shape(F, WIDTH),) * 2,
        [SMEM] + [VMEM] * 4,
        (VMEM,) * 2,
        size=1 << 20,
    )
    return attended, grad_queries, grad_keys, grad_values


def solution(mesh):
    sharded = P("tm", None, None)
    return jax.shard_map(
        step,
        mesh=mesh,
        in_specs=(sharded,) * 4 + (P(),),
        out_specs=(sharded,) * 4,
        check_vma=False,
    )
```

```python
import jax
import jax.numpy as jnp
from jax import lax
from jax.experimental import pallas as pl
from jax.experimental.pallas import tpu as pltpu
from jax.sharding import PartitionSpec as P


HEADS = 10
F = 4
C = 2 * F
REACH = 3
HALO = C
REMOTE = C + 1
SLOTS = C + 2
SIZE = 64
STEP = 256
SPAN = 384
REST = 256
WIDTH = HEADS * SIZE
F32 = jnp.float32
BF16 = jnp.bfloat16
VMEM = pl.BlockSpec(memory_space=pltpu.VMEM)
SMEM = pl.BlockSpec(memory_space=pltpu.SMEM)
HBM = pl.BlockSpec(memory_space=pltpu.HBM)
LIMIT = pltpu.CompilerParams(vmem_limit_bytes=20 << 20)

OWN, PREV, BACK, OPEN, TAKE, META = 0, C, 2 * C, 2 * C + 1, 2 * C + 2, 2 * C + 2 + REACH


def ring(value, steps):
    count = lax.axis_size("tm")
    return lax.ppermute(value, "tm", [(s, (s + steps) % count) for s in range(count)])


def swap(value):
    count = lax.axis_size("tm")
    return lax.ppermute(value, "tm", [(s, s ^ 1) for s in range(count)])


def place():
    device = lax.axis_index("tm")
    return lax.shift_right_logical(device, 1), device & 1


def window(core):
    return pl.ds(pl.multiple_of(core * STEP, 128), SPAN)


def prep_kernel(clips_ref, keys_ref, values_ref, meta_ref, mine_ref, send_ref, lengths_ref, frames, sems):
    count = pltpu.make_async_copy(clips_ref, lengths_ref, sems.at[2])
    count.start()
    copies = [
        pltpu.make_async_copy(ref, frames.at[i], sems.at[i])
        for i, ref in enumerate((keys_ref, values_ref))
    ]
    for copy in copies:
        copy.start()
    chip, core = place()
    first = chip * C
    total = lax.axis_size("tm") * F
    clips = lengths_ref.shape[1]
    rows = lax.broadcasted_iota(jnp.int32, (clips, clips), 0)
    columns = lax.broadcasted_iota(jnp.int32, (clips, clips), 1)
    earlier = jnp.where(rows < columns, 1.0, 0.0).astype(BF16)
    count.wait()
    lengths = jnp.broadcast_to(lengths_ref[...].astype(F32), (16, clips)).astype(BF16)
    starts = jnp.dot(lengths, earlier, preferred_element_type=F32)[:1].astype(jnp.int32)

    def owner_of(frame):
        return jnp.max(jnp.where(starts <= frame, starts, 0))

    owners = [owner_of(first + i) for i in range(C)]
    for i in range(C):
        local = owners[i] - first
        meta_ref[OWN + i] = jnp.where(local >= 0, local, REMOTE)
        meta_ref[PREV + i] = jnp.where(local == i, i, i - 1 if i else HALO)
    meta_ref[BACK] = jnp.clip(chip - lax.shift_right_logical(owners[0], 3), 1, REACH)
    opened = owners[C - 1] - first
    meta_ref[OPEN] = opened
    for k in range(1, REACH + 1):
        ahead = first + C * k
        owner = owner_of(ahead) - first
        mine = (owner >= 0) & (owner < C) & (ahead < total)
        meta_ref[TAKE + k - 1] = mine.astype(jnp.int32)
    local = opened - core * F
    holds = (local >= 0) & (local < F)
    frame = jnp.clip(local, 0, F - 1)
    for copy in copies:
        copy.wait()
    for target, columns in ((mine_ref, window(core)), (send_ref, window(1 - core))):
        for i in range(2):
            target[i] = jnp.where(holds, frames[i, frame, :, columns], 0).astype(BF16)
            target[2 + i] = jnp.where(core == 1, frames[i, F - 1, :, columns], 0).astype(BF16)


def pack_kernel(q_ref, keys_ref, values_ref, g_ref, after_ref, mine_ref, send_ref, sems):
    core = place()[1]
    copies = []
    for t, (target, side) in enumerate(((send_ref, 1 - core), (mine_ref, core))):
        for i, ref in enumerate((q_ref, keys_ref, values_ref, g_ref)):
            copies.append(
                pltpu.make_async_copy(
                    ref.at[:, :, window(side)], target.at[pl.ds(i * F, F)], sems.at[4 * t + i]
                )
            )
    for copy in copies:
        copy.start()
    for copy in copies:
        copy.wait()


UNITS = C + C // 2
UNIT = 4 * SIZE
HALF = UNIT // 2


def frames_of(unit):
    return (unit,) if unit < C else (2 * (unit - C), 2 * (unit - C) + 1)


def unit_of(load, unit):
    if unit < C:
        return load(unit, slice(0, UNIT))
    return jnp.concatenate([load(i, slice(UNIT, SPAN)) for i in frames_of(unit)], axis=1)


def spread(block):
    lane = lax.broadcasted_iota(jnp.int32, block.shape, 1)
    parts = [
        jnp.where((lane >= start) & (lane < start + SIZE), block, jnp.zeros_like(block))
        for start in range(0, block.shape[1], SIZE)
    ]
    return jnp.concatenate(parts, axis=0)


def fold(product):
    heads = product.shape[1] // SIZE
    tokens = product.shape[0] // heads
    lane = lax.broadcasted_iota(jnp.int32, (tokens, HALF), 1)
    parts = []
    for start in range(0, product.shape[1], HALF):
        h = start // SIZE
        columns = slice(start, start + HALF)
        low = product[h * tokens : (h + 1) * tokens, columns]
        high = product[(h + 1) * tokens : (h + 2) * tokens, columns]
        parts.append(jnp.where(lane < SIZE, low, high))
    return jnp.concatenate(parts, axis=1)


def contract(a, b, da, db):
    return lax.dot_general(a, b, (((da,), (db,)), ((), ())), preferred_element_type=F32)


SCALE = SIZE ** (-0.5)


EDGES = (0, C)


def local_kernel(
    meta_ref, mine_ref, theirs_ref, qs, gs, own_k, own_v, prev_k, prev_v, e_prev, d_prev, stats, qt, gt, slots
):
    core = place()[1]
    for source, base in ((mine_ref, core * F), (theirs_ref, (1 - core) * F)):
        for a in range(4):
            for j in range(F):
                slots[a, base + j] = source[a * F + j]
    own = [jnp.minimum(meta_ref[OWN + i], C - 1) for i in range(C)]
    prev = [jnp.minimum(meta_ref[PREV + i], C - 1) for i in range(C)]
    for u in range(UNITS):
        q = spread(unit_of(lambda i, columns: slots[0, i, :, columns], u) * jnp.asarray(SCALE, BF16))
        g = spread(unit_of(lambda i, columns: slots[3, i, :, columns], u))
        qs[u], gs[u] = q, g
        qt[u], gt[u] = q.T, g.T
        own_k[u] = unit_of(lambda i, columns: slots[1, own[i], :, columns], u)
        own_v[u] = unit_of(lambda i, columns: slots[2, own[i], :, columns], u)
        prev_k[u] = unit_of(lambda i, columns: slots[1, prev[i], :, columns], u)
        prev_v[u] = unit_of(lambda i, columns: slots[2, prev[i], :, columns], u)
    for u in range(UNITS):
        if u in EDGES:
            continue
        scores = contract(prev_k[u], qt[u], 1, 0)
        grad_prob = contract(prev_v[u], gt[u], 1, 0)
        top = jnp.max(scores, axis=0, keepdims=True)
        expos = jnp.exp(scores - top)
        e_prev[u] = expos
        d_prev[u] = grad_prob
        stats[u, 0:1] = top
        stats[u, 1:2] = jnp.sum(expos, axis=0, keepdims=True)
        stats[u, 2:3] = jnp.sum(expos * grad_prob, axis=0, keepdims=True)


def farther(meta_ref, r1, r2, r3, which):
    back = meta_ref[BACK]
    return jnp.where(back == 1, r1[which], jnp.where(back == 2, r2[which], r3[which]))


def own_rows(meta_ref, local, far, u):
    def load(i, columns):
        here = local[u] if u < C else local[u, :, (i % 2) * HALF : (i % 2 + 1) * HALF]
        return jnp.where(meta_ref[OWN + i] == REMOTE, far[:, columns], here)

    return unit_of(load, u)


def prev_rows(meta_ref, local, halo, u):
    if u not in (0, C):
        return local[u]
    outside = meta_ref[PREV] == HALO
    if u == 0:
        return jnp.where(outside, halo[:, :UNIT], local[u])
    left = jnp.where(outside, halo[:, UNIT:], local[u, :, :HALF])
    return jnp.concatenate([left, local[u, :, HALF:]], axis=1)


def near_kernel(
    meta_ref, r1, r2, r3, qs, gs, own_k, own_v, prev_k, prev_v, stats, qt, gt,
    sums_ref, edge_ref, prob_ref, grad_ref, first_ref, merged_ref,
):
    tokens = r1.shape[1]
    far_k, far_v = farther(meta_ref, r1, r2, r3, 0), farther(meta_ref, r1, r2, r3, 1)
    lane = lax.broadcasted_iota(jnp.int32, (tokens, UNIT // 2), 1)

    def total(block):
        return jnp.sum(block, axis=0, keepdims=True)

    def kept(block, u):
        flags = [meta_ref[OWN + i] == REMOTE for i in frames_of(u)]
        if u < C:
            return jnp.where(flags[0], block, jnp.zeros_like(block))
        inside = ((lane < SIZE) & flags[0]) | ((lane >= SIZE) & flags[1])
        return jnp.where(inside, block, jnp.zeros_like(block))

    def products(u):
        score = contract(own_rows(meta_ref, own_k, far_k, u), qt[u], 1, 0)
        grad_prob = contract(own_rows(meta_ref, own_v, far_v, u), gt[u], 1, 0)
        if u not in EDGES:
            return score, grad_prob
        before = contract(prev_rows(meta_ref, prev_k, r1[2], u), qt[u], 1, 0)
        grad_before = contract(prev_rows(meta_ref, prev_v, r1[3], u), gt[u], 1, 0)
        return score, grad_prob, before, grad_before

    def softened(u, score, grad_prob, before=None, grad_before=None):
        top = jnp.max(score, axis=0, keepdims=True)
        if u in EDGES:
            n = EDGES.index(u)
            top = jnp.maximum(top, jnp.max(before, axis=0, keepdims=True))
            expos, earlier = jnp.exp(score - top), jnp.exp(before - top)
            inverse = 1.0 / (total(expos) + total(earlier))
            inner = (total(expos * grad_prob) + total(earlier * grad_before)) * inverse
            prob = earlier * inverse
            first_ref[n, 0] = prob.astype(BF16)
            first_ref[n, 1] = (prob * (grad_before - inner)).astype(BF16)
        else:
            older = stats[u, 0:1]
            top = jnp.maximum(top, older)
            expos, rescale = jnp.exp(score - top), jnp.exp(older - top)
            inverse = 1.0 / (total(expos) + rescale * stats[u, 1:2])
            inner = (total(expos * grad_prob) + rescale * stats[u, 2:3]) * inverse
            merged_ref[u, 0:1] = rescale * inverse
            merged_ref[u, 1:2] = inner
        prob = expos * inverse
        low = prob.astype(BF16)
        low_grad = (prob * (grad_prob - inner)).astype(BF16)
        prob_ref[u] = low
        grad_ref[u] = low_grad
        return kept(low_grad, u), kept(low, u)

    halo = meta_ref[PREV] == HALO
    sums = [[None, None], [None, None]]
    ahead = 12
    ready = {u: products(u) for u in range(ahead)}
    for u in range(0, UNITS, 2):
        soft = [softened(v, *ready.pop(v)) for v in (u, u + 1)]
        for v in range(u + ahead, min(u + ahead + 2, UNITS)):
            ready[v] = products(v)
        part = int(u >= C)
        for j, other in enumerate((qs, gs)):
            left = jnp.concatenate([soft[0][j], soft[1][j]], axis=1)
            right = other[u : u + 2].reshape(UNIT, UNIT)
            product = contract(left, right, 1, 0)
            sums[j][part] = product if sums[j][part] is None else sums[j][part] + product
    for j, other in enumerate((qs, gs)):
        pairs = sums[j][1]
        rest = (pairs[:, :HALF] + pairs[:, HALF:]).astype(BF16)
        for target in (sums_ref, edge_ref):
            target[j, :, :UNIT] = sums[j][0].astype(BF16)
            target[j, :, UNIT:] = rest
        left = contract(first_ref[0, 1 - j], other[0], 1, 0)
        right = contract(first_ref[1, 1 - j], other[C], 1, 0)[:, :HALF]
        edge_ref[2 + j, :, :UNIT] = jnp.where(halo, left, 0.0).astype(BF16)
        edge_ref[2 + j, :, UNIT:] = jnp.where(halo, right, 0.0).astype(BF16)


def full_kernel(
    meta_ref, r1, r2, r3, qs, gs, own_k, own_v, prev_k, prev_v, e_prev, d_prev,
    prob_ref, grad_ref, first_ref, merged_ref, keep_ref, send_ref, touch_ref, out, key_part, value_part, key_sum, value_sum,
):
    tokens = r1.shape[1]
    far_k, far_v = farther(meta_ref, r1, r2, r3, 0), farther(meta_ref, r1, r2, r3, 1)

    def place_unit(target, base, u, rows, block):
        if u < C:
            target[base + u, rows, :UNIT] = block
        else:
            for n, i in enumerate(frames_of(u)):
                target[base + i, rows, UNIT:] = block[:, n * HALF : (n + 1) * HALF]

    everything = slice(None)
    for u in range(UNITS):
        key = jnp.concatenate(
            [own_rows(meta_ref, own_k, far_k, u), prev_rows(meta_ref, prev_k, r1[2], u)], axis=0
        )
        value = jnp.concatenate(
            [own_rows(meta_ref, own_v, far_v, u), prev_rows(meta_ref, prev_v, r1[3], u)], axis=0
        )
        if u in EDGES:
            n = EDGES.index(u)
            before, grad_before = first_ref[n, 0], first_ref[n, 1]
        else:
            wide = e_prev[u] * merged_ref[u, 0:1]
            before = wide.astype(BF16)
            grad_before = (wide * (d_prev[u] - merged_ref[u, 1:2])).astype(BF16)
        prob = jnp.concatenate([prob_ref[u], before], axis=0)
        grad = jnp.concatenate([grad_ref[u], grad_before], axis=0)
        attended = fold(contract(prob, value, 0, 0)).astype(BF16)
        grad_q = (fold(contract(grad, key, 0, 0)) * SCALE).astype(BF16)
        place_unit(out, 0, u, everything, attended)
        place_unit(out, C, u, everything, grad_q)
        place_unit(value_part, 0, u, everything, contract(prob, gs[u], 1, 0))
        place_unit(key_part, 0, u, everything, contract(grad, qs[u], 1, 0))
    for part, total in ((key_part, key_sum), (value_part, value_sum)):
        for i in range(C):
            here = jnp.where(meta_ref[PREV + i] == i, part[i, tokens:], 0.0)
            if i + 1 < C:
                here += jnp.where(meta_ref[PREV + i + 1] == i, part[i + 1, tokens:], 0.0)
            total[i] = here
    for i in range(C):
        own = meta_ref[OWN + i]
        key_sum[own] += key_part[i, :tokens]
        value_sum[own] += value_part[i, :tokens]
    for i in range(C):
        out[2 * C + i] = key_sum[i].astype(BF16)
        out[3 * C + i] = value_sum[i].astype(BF16)
    opened = jnp.maximum(meta_ref[OPEN], 0)
    touch_ref[0] = key_sum[opened]
    touch_ref[1] = value_sum[opened]
    touch_ref[2] = key_sum[C - 1]
    touch_ref[3] = value_sum[C - 1]
    core = place()[1]
    lacking = pl.ds(pl.multiple_of(core * 128, 128), REST)
    for a in range(4):
        for j in range(F):
            keep_ref[a * F + j] = out[a * C + core * F + j]
            send_ref[a * F + j] = out[a * C + (1 - core) * F + j, :, lacking]


def join(core, target, kept, got):
    @pl.when(core == 0)
    def _():
        target[:, :SPAN] = kept
        target[:, SPAN:] = got

    @pl.when(core == 1)
    def _():
        target[:, :STEP] = got
        target[:, STEP:] = kept


def early_kernel(keep_ref, got_ref, attended_ref, grad_q_ref):
    core = place()[1]
    for a, target in enumerate((attended_ref, grad_q_ref)):
        for j in range(F):
            join(core, target.at[j], keep_ref[a * F + j], got_ref[a * F + j])


def touch_kernel(meta_ref, touch_ref, r1, r2, r3, kept_ref, send_ref):
    core = place()[1]
    lacking = pl.ds(pl.multiple_of(core * 128, 128), REST)
    same = meta_ref[OPEN] == C - 1
    for a in range(2):
        edge = r1[2 + a].astype(F32)
        total = touch_ref[a] + jnp.where(same, edge, 0.0)
        for k, r in enumerate((r1, r2, r3)):
            total += jnp.where(meta_ref[TAKE + k] > 0, r[a].astype(F32), 0.0)
        kept_ref[a] = total.astype(BF16)
        kept_ref[2 + a] = (touch_ref[2 + a] + edge).astype(BF16)
    for a in range(4):
        send_ref[a] = kept_ref[a, :, lacking]


def final_kernel(meta_ref, keep_ref, got_ref, touched_ref, touched_got_ref, grad_keys_ref, grad_values_ref):
    core = place()[1]
    local = meta_ref[OPEN] - core * F
    for a, target in enumerate((grad_keys_ref, grad_values_ref)):
        for j in range(F):
            join(core, target.at[j], keep_ref[(2 + a) * F + j], got_ref[(2 + a) * F + j])

        @pl.when(core == 1)
        def _():
            join(core, target.at[F - 1], touched_ref[2 + a], touched_got_ref[2 + a])

        @pl.when((local >= 0) & (local < F))
        def _():
            join(core, target.at[local], touched_ref[a], touched_got_ref[a])


def call(kernel, operands, outs, in_specs, out_specs, scratch=(), flops=0, size=0):
    return pl.pallas_call(
        kernel,
        out_shape=outs,
        in_specs=in_specs,
        out_specs=out_specs,
        scratch_shapes=list(scratch),
        compiler_params=LIMIT,
        cost_estimate=pl.CostEstimate(flops=flops, bytes_accessed=size, transcendentals=0),
    )(*operands)


def step(queries, keys, values, out_grad, clip_lengths):
    tokens = queries.shape[1]
    queries, keys, values, out_grad = (
        pltpu.with_memory_space_constraint(a, pltpu.HBM) for a in (queries, keys, values, out_grad)
    )

    def shape(count, columns, dtype=BF16):
        return jax.ShapeDtypeStruct((count, tokens, columns), dtype)

    def room(count, dtype=BF16):
        return pltpu.VMEM((count, tokens, SPAN), dtype)

    meta, own_edge, send_edge = call(
        prep_kernel,
        (pltpu.with_memory_space_constraint(clip_lengths.reshape(1, -1), pltpu.HBM), keys, values),
        (jax.ShapeDtypeStruct((META,), jnp.int32), shape(4, SPAN), shape(4, SPAN)),
        [HBM, HBM, HBM],
        (SMEM, VMEM, VMEM),
        [
            pltpu.VMEM((1, clip_lengths.shape[0]), jnp.int32),
            pltpu.VMEM((2, F, tokens, WIDTH), BF16),
            pltpu.SemaphoreType.DMA((3,)),
        ],
        size=1 << 20,
    )
    got_edge = swap(send_edge)
    edge = own_edge + got_edge
    opened = own_edge[:2] + got_edge[:2]
    far = ring(opened, 6), ring(opened, 4)
    received = (ring(edge, 2), far[1], far[0])
    mine, send = call(
        pack_kernel,
        (queries, keys, values, out_grad, edge),
        (shape(4 * F, SPAN), shape(4 * F, SPAN)),
        [HBM] * 4 + [VMEM],
        (VMEM, VMEM),
        [pltpu.SemaphoreType.DMA((8,))],
        size=2 << 20,
    )
    theirs = swap(send)
    wide = jax.ShapeDtypeStruct((UNITS, UNIT // 2, UNIT), BF16)
    rows = jax.ShapeDtypeStruct((UNITS, tokens, UNIT), BF16)
    lanes = UNIT // 2
    half = jax.ShapeDtypeStruct((UNITS, tokens, lanes), F32)
    tall = jax.ShapeDtypeStruct((UNITS, UNIT, lanes), BF16)
    few = jax.ShapeDtypeStruct((UNITS, 8, lanes), F32)
    local = call(
        local_kernel,
        (meta, mine, theirs),
        (wide, wide, rows, rows, rows, rows, half, half, few, tall, tall),
        [SMEM] + [VMEM] * 2,
        (VMEM,) * 11,
        [pltpu.VMEM((4, C, tokens, SPAN), BF16)],
        size=4 << 20,
    )
    soft = jax.ShapeDtypeStruct((UNITS, tokens, lanes), BF16)
    first = jax.ShapeDtypeStruct((2, 2, tokens, lanes), BF16)
    flops = 24 * C * tokens * tokens * SPAN
    sums, edge_sums, *softened = call(
        near_kernel,
        (meta, *received, *local[:6], *local[8:]),
        (shape(2, SPAN), shape(4, SPAN), soft, soft, first, few),
        [SMEM] + [VMEM] * 12,
        (VMEM,) * 6,
        [],
        flops,
        2 << 20,
    )
    far = ring(sums, -6), ring(sums, -4)
    returned = (ring(edge_sums, -2), far[1], far[0])
    keep, send_out, touch = call(
        full_kernel,
        (meta, *received, *local[:8], *softened),
        (shape(4 * F, SPAN), shape(4 * F, REST), shape(4, SPAN, F32)),
        [SMEM] + [VMEM] * 15,
        (VMEM,) * 3,
        [room(4 * C)]
        + [pltpu.VMEM((C, 2 * tokens, SPAN), F32)] * 2
        + [room(SLOTS, F32), room(SLOTS, F32)],
        4 * flops,
        4 << 20,
    )
    got_out = swap(send_out)
    attended, grad_queries = call(
        early_kernel, (keep, got_out), (shape(F, WIDTH),) * 2, [VMEM] * 2, (VMEM,) * 2, size=1 << 20
    )
    touched, send_touched = call(
        touch_kernel,
        (meta, touch, *returned),
        (shape(4, SPAN), shape(4, REST)),
        [SMEM] + [VMEM] * 4,
        (VMEM,) * 2,
        size=1 << 20,
    )
    grad_keys, grad_values = call(
        final_kernel,
        (meta, keep, got_out, touched, swap(send_touched)),
        (shape(F, WIDTH),) * 2,
        [SMEM] + [VMEM] * 4,
        (VMEM,) * 2,
        size=1 << 20,
    )
    return attended, grad_queries, grad_keys, grad_values


def solution(mesh):
    sharded = P("tm", None, None)
    return jax.shard_map(
        step,
        mesh=mesh,
        in_specs=(sharded,) * 4 + (P(),),
        out_specs=(sharded,) * 4,
        check_vma=False,
    )
```
